512 devices in a mesh: tx: 32 (over x, z), ty: 16 (over y, core).
Axes of the slice: x: 4, y: 8, z: 8, core: 2. Of those that a mesh axis runs over, the one named last changes fastest.
Arguments:
- features: bfloat16 [2048, 128, 128], P(('tx', 'ty')), may hold values from -6 to 6
- occupancy: int32 [2048, 128], P(('tx', 'ty')), may hold values from 0 to 1, as said below
- neighbors: int32 [27, 2048], P(None, ('tx', 'ty')), may hold values from -1 to 2047, as said below
- point_voxel: int32 [524288], P(('tx', 'ty')), may hold values from 0 to 511, as said below
- conv_weight: bfloat16 [27, 128, 128], replicated, may hold values from -0.109375 to 0.109375
- head_weight: bfloat16 [16, 128], replicated, may hold values from -0.5 to 0.5
- teacher: bfloat16 [16, 524288], P(None, ('tx', 'ty')), may hold values from -15 to 15
Outputs:
- grad_features: bfloat16 [2048, 128, 128], P(('tx', 'ty'))
- grad_weight: float32 [27, 128, 128], replicated
The draws below stay inside these ranges and needn't reach their ends.
Inputs may be any that keep to these rules, and one draw needn't show every extreme that they name: `occupancy`: every voxel of a slot that holds no active brick is 0; every active brick has one or more occupied voxels. A brick's global slot is 4 times its tile's index (tx index times the number of ty devices plus ty index) plus (2 i + j) + k for its place (i, j, k) in the tile's 2 x 2 x 1 grid of bricks. neighbors[o, b] is the global slot of the brick at brick offset o from b if that brick is active and b is active, else -1; neighbors[13, b] is b exactly when b is active. At most 3 bricks of a tile are active, and some tile has exactly 3. `point_voxel`: each entry is 128 s + v for an occupied voxel v of slot s of the point's own tile.
All inputs are finite; a program needn't handle non-finite values.
Results may differ from the reference program's by a relative error of at most 0.0052.
Values may be sent and summed in bfloat16 or wider, within the bound.
A program may use at most 64 MiB of HBM per device.

```python
import jax
import jax.numpy as jnp
from jax import lax

C = 128
K = 16
GX = 2
GY = 2
GZ = 1
POINTS_DEV = 1024
TILE_POS = 4
ACTIVE_MAX = 3
BRICKS = 2048
POINTS = 524288
N_TX = 32
N_TY = 16


def layout_draw(key):
    base_key = jax.random.fold_in(key, 7)
    key_count, key_full, key_order, key_occupy, key_keep = jax.random.split(base_key, 5)
    tile_count = N_TX * N_TY
    uniform_pick = jax.random.randint(key_count, (tile_count,), 0, ACTIVE_MAX + 1)
    counts = jnp.minimum(ACTIVE_MAX, jnp.maximum(2, uniform_pick))
    fullest = jax.random.randint(key_full, (), 0, tile_count)
    counts = jnp.where(jnp.arange(tile_count) == fullest, ACTIVE_MAX, counts)
    scores = jax.random.randint(key_order, (tile_count, TILE_POS), 0, 1 << 30)
    scores = scores.at[tile_count - 1, TILE_POS - 1].set(-1)
    slot_order = jnp.argsort(scores, axis=1, stable=True)
    slot_ranks = jnp.argsort(slot_order, axis=1, stable=True)
    active = (slot_ranks < counts[:, None]).astype(jnp.int32)
    bricks = tile_count * TILE_POS
    filled = (jax.random.randint(key_occupy, (bricks, 128), 0, 8) < 5).astype(jnp.int32)
    single = jax.random.randint(key_keep, (bricks, 1), 0, 128)
    filled = jnp.maximum(filled, (jnp.arange(128)[None, :] == single).astype(jnp.int32))
    filled = filled.at[bricks - 1, 127].set(1)
    occupancy = filled * active.reshape(bricks, 1)
    return (active, occupancy)


def draw_occupancy(key, part):
    return layout_draw(key)[1].astype(jnp.int32)


def draw_neighbors(key, part):
    active, occupancy = layout_draw(key)
    tile_count = N_TX * N_TY
    bricks = tile_count * TILE_POS
    brick_ids = jnp.arange(bricks)
    tile_ids = brick_ids // TILE_POS
    places = brick_ids % TILE_POS
    coord_x = tile_ids // N_TY * GX + places // (GY * GZ)
    coord_y = tile_ids % N_TY * GY + places // GZ % GY
    coord_z = places % GZ
    active_flat = active.reshape(bricks)
    rows_list = []
    for move_x in (-1, 0, 1):
        for move_y in (-1, 0, 1):
            for move_z in (-1, 0, 1):
                near_x = coord_x + move_x
                near_y = coord_y + move_y
                near_z = coord_z + move_z
                inside = (near_x >= 0) & (near_x < N_TX * GX) & (near_y >= 0) & (near_y < N_TY * GY) & (near_z >= 0) & (near_z < GZ)
                safe_x = jnp.clip(near_x, 0, N_TX * GX - 1)
                safe_y = jnp.clip(near_y, 0, N_TY * GY - 1)
                safe_z = jnp.clip(near_z, 0, GZ - 1)
                near_tile = safe_x // GX * N_TY + safe_y // GY
                near_place = (safe_x % GX * GY + safe_y % GY) * GZ + safe_z
                near_id = near_tile * TILE_POS + near_place
                usable = inside & (active_flat[near_id] > 0) & (active_flat > 0)
                rows_list.append(jnp.where(usable, near_id, -1))
    return jnp.stack(rows_list).astype(jnp.int32)


def locate(running_row, wanted):
    return jnp.searchsorted(running_row, wanted, side='left')


def draw_point_voxel(key, part):
    active, occupancy = layout_draw(key)
    tile_count = N_TX * N_TY
    per_tile = occupancy.reshape(tile_count, TILE_POS * 128)
    running = jnp.cumsum(per_tile, axis=1)
    totals = running[:, -1]
    picks = jax.random.randint(jax.random.fold_in(key, 11), (tile_count, POINTS_DEV), 0, 1 << 30)
    wanted = picks % totals[:, None] + 1
    voxels = jax.vmap(locate)(running, wanted)
    voxels = voxels.at[tile_count - 1, POINTS_DEV - 1].set(TILE_POS * 128 - 1)
    return voxels.reshape(-1).astype(jnp.int32)


def block_levels(own_key, shape, cuts, low, largest):
    def one(position, shards_of):
        steps = jax.random.uniform(jax.random.fold_in(jax.random.fold_in(own_key, 6), position), (shards_of,), jnp.float32, low / len(cuts), largest / len(cuts))
        return jnp.repeat(jnp.exp(steps), shape[position] // shards_of).reshape((-1,) + (1,) * (len(shape) - position - 1))

    gain = one(*cuts[0])
    for cut in cuts[1:]:
        gain = gain * one(*cut)
    return gain


def centred(key, shape, width, reach, shards=(), dtype=jnp.bfloat16):
    entries = width * jax.random.normal(key, shape, jnp.float32)
    if shards:
        entries = entries * block_levels(key, shape, shards, -0.22, 0.18)
    return jnp.clip(entries, -reach, reach).astype(dtype)


def setup_inputs(seed: int = 0) -> dict:
    keys = jax.random.split(jax.random.key(seed), 8)
    return {
        "features": centred(keys[0], (BRICKS, 128, C), 1.0, 6.0, ((0, 512),)),
        "occupancy": draw_occupancy(jax.random.fold_in(keys[7], 71), 0),
        "neighbors": draw_neighbors(jax.random.fold_in(keys[7], 71), 0),
        "point_voxel": draw_point_voxel(jax.random.fold_in(keys[7], 71), 0),
        "conv_weight": centred(keys[4], (27, C, C), (27 * C) ** -0.5, 0.109375),
        "head_weight": centred(keys[5], (K, C), C ** -0.5, 0.5),
        "teacher": centred(keys[6], (K, POINTS), 3.0, 15.0, ((1, 512),)),
    }


def span_of(move, length):
    if move < 0:
        return (length - 1, length)
    if move == 0:
        return (0, length)
    return (0, 1)

def assemble_blocks(table, index):
    planes = []
    for move_x in (-1, 0, 1):
        columns = []
        for move_y in (-1, 0, 1):
            pieces = []
            for move_z in (-1, 0, 1):
                offset = 9 * (move_x + 1) + 3 * (move_y + 1) + (move_z + 1)
                start_x, stop_x = span_of(move_x, 4)
                start_y, stop_y = span_of(move_y, 4)
                start_z, stop_z = span_of(move_z, 8)
                window = table[:, start_x:stop_x, start_y:stop_y, start_z:stop_z, :]
                pieces.append(jnp.take(window, index[offset], axis=0))
            columns.append(jnp.concatenate(pieces, axis=3))
        planes.append(jnp.concatenate(columns, axis=2))
    return jnp.concatenate(planes, axis=1)

def plane_columns(padded, move_x, transpose):
    channels = padded.shape[-1]
    windows = []
    for move_y in (-1, 0, 1):
        for move_z in (-1, 0, 1):
            if transpose:
                anchor = (1 - move_x, 1 - move_y, 1 - move_z)
            else:
                anchor = (1 + move_x, 1 + move_y, 1 + move_z)
            window = padded[:, anchor[0]:anchor[0] + 4, anchor[1]:anchor[1] + 4, anchor[2]:anchor[2] + 8, :]
            windows.append(window.reshape(-1, channels))
    return jnp.concatenate(windows, axis=1)

def convolve(padded, weight, transpose):
    channels = padded.shape[-1]
    summed = jnp.zeros((padded.shape[0] * 128, channels), jnp.float32)
    for move_x in (-1, 0, 1):
        first = 9 * (move_x + 1)
        if transpose:
            matrix = jnp.concatenate([weight[first + inner].T for inner in range(9)], axis=0)
        else:
            matrix = weight[first:first + 9].reshape(9 * channels, channels)
        columns = plane_columns(padded, move_x, transpose)
        summed = summed + jnp.dot(columns, matrix, preferred_element_type=jnp.float32)
    return summed

def weight_terms(padded, gradient):
    channels = padded.shape[-1]
    flat_grad = gradient.reshape(-1, channels)
    terms = []
    for move_x in (-1, 0, 1):
        columns = plane_columns(padded, move_x, False)
        product = lax.dot_general(columns, flat_grad, (((0,), (0,)), ((), ())), preferred_element_type=jnp.float32)
        terms.append(product.reshape(9, channels, channels))
    return jnp.concatenate(terms, axis=0)

def silu_slope(value):
    logistic = jax.nn.sigmoid(value)
    return logistic * (1.0 + value * (1.0 - logistic))

def tile_gradient(pre, occupied, voxel_index, teacher_block, head_weight):
    channels = pre.shape[-1]
    occupied_cells = occupied[..., None]
    hidden = (jax.nn.silu(pre) * occupied_cells).astype(jnp.bfloat16)
    chosen = jnp.take(hidden.reshape(-1, channels), voxel_index, axis=0)
    logits = lax.dot_general(head_weight, chosen, (((1,), (1,)), ((), ())), preferred_element_type=jnp.float32)
    student = jnp.exp(logits)
    student = student / lax.optimization_barrier(jnp.sum(student, axis=0, keepdims=True))
    target = jnp.exp(teacher_block.astype(jnp.float32))
    target = target / lax.optimization_barrier(jnp.sum(target, axis=0, keepdims=True))
    slope_logits = student - target
    per_point = jnp.dot(slope_logits.T, head_weight.astype(jnp.float32), precision=lax.Precision.HIGHEST)
    per_voxel = jnp.zeros((pre.shape[0] * 128, channels), jnp.float32).at[voxel_index].add(per_point)
    return (per_voxel.reshape(pre.shape) * silu_slope(pre) * occupied_cells).astype(jnp.bfloat16)

def reference(features, occupancy, neighbors, point_voxel, conv_weight, head_weight, teacher):
    tile_count = N_TX * N_TY
    masked = features * occupancy.astype(jnp.bfloat16)[..., None]
    zero_brick = jnp.zeros((1, 4, 4, 8, C), jnp.bfloat16)
    table_x = jnp.concatenate([masked.reshape(BRICKS, 4, 4, 8, C), zero_brick], axis=0)
    index_all = jnp.where(neighbors < 0, BRICKS, neighbors).astype(jnp.int32)
    index_tiles = index_all.reshape(27, tile_count, TILE_POS).transpose(1, 0, 2)
    occupied_tiles = occupancy.reshape(tile_count, TILE_POS, 128).astype(jnp.float32)
    voxel_tiles = point_voxel.reshape(tile_count, POINTS_DEV).astype(jnp.int32)
    teacher_tiles = teacher.reshape(K, tile_count, POINTS_DEV).transpose(1, 0, 2)

    def forward_tile(inputs):
        index, occupied, voxel_index, teacher_block = inputs
        padded = assemble_blocks(table_x, index)
        pre = convolve(padded, conv_weight, False).reshape(TILE_POS, 128, C)
        return tile_gradient(pre, occupied, voxel_index, teacher_block, head_weight)
    gradient = lax.map(forward_tile, (index_tiles, occupied_tiles, voxel_tiles, teacher_tiles))
    table_g = jnp.concatenate([gradient.reshape(BRICKS, 4, 4, 8, C), zero_brick], axis=0)

    def backward_tile(carry, inputs):
        index, occupied, tile_grad = inputs
        padded_g = assemble_blocks(table_g, index)
        back_sum = convolve(padded_g, conv_weight, True).reshape(TILE_POS, 128, C)
        result = (back_sum * occupied[..., None]).astype(jnp.bfloat16)
        padded_x = assemble_blocks(table_x, index)
        return (carry + weight_terms(padded_x, tile_grad), result)
    summed, grad_tiles = lax.scan(backward_tile, jnp.zeros((27, C, C), jnp.float32), (index_tiles, occupied_tiles, gradient))
    grad_weight = summed / jnp.sqrt(jnp.mean(summed * summed) + 1e-06)
    return (grad_tiles.reshape(BRICKS, 128, C), grad_weight)
```

```python
import functools

import jax
import jax.numpy as jnp
from jax import lax
from jax.experimental import pallas as pl
from jax.experimental.pallas import tpu as pltpu
from jax.sharding import PartitionSpec as P

F32 = jnp.float32
BF16 = jnp.bfloat16
MESH = pl.DeviceIdType.MESH
ROUTES = ((-1, 0), (1, 0), (0, -1), (0, 1), (-1, -1), (-1, 1), (1, -1), (1, 1))
HALF = 14
TN = (((0,), (0,)), ((), ()))
NT = (((1,), (1,)), ((), ()))


def span_to_send(step):
    if step < 0:
        return slice(1, 2)
    if step > 0:
        return slice(8, 9)
    return slice(1, 9)


def span_received(step):
    if step < 0:
        return slice(9, 10)
    if step > 0:
        return slice(0, 1)
    return slice(1, 9)


def split3(value):
    one = value.astype(BF16)
    rest = value - one.astype(F32)
    two = rest.astype(BF16)
    three = (rest - two.astype(F32)).astype(BF16)
    return one, two, three


def kernel(
    sizes,
    near_ref, occ_ref, feat_ref, point_ref, weight_hbm, head_ref, teacher_ref,
    grad_ref, sum_ref, norm_ref,
    cells, occ_cells, columns, columns_g, weight, weight_t, halo_out, halo_in,
    terms, pair_out, pair_in, ring_out, ring_in, mid, mid_in, row_out, row_in, last, full,
    weight_sem, halo_send, halo_recv, pair_send, pair_recv, ring_send, ring_recv,
    mid_send, mid_recv, row_send, row_recv, thin_send, thin_recv,
    wide_send, wide_recv, core_send, core_recv,
):
    nx, ring, per, used = sizes
    rows = 64 // ring
    n_tx = nx * ring
    n_ty = 2 * ring
    tx = lax.axis_index("tx")
    ty = lax.axis_index("ty")
    place_x, place_z = tx // ring, tx % ring
    place_y, core = ty // 2, ty % 2

    def along_x(d):
        return (((place_x + d) % nx) * ring + place_z, ty)

    def along_z(d):
        return (place_x * ring + (place_z + d) % ring, ty)

    def along_y(d):
        return (tx, ((place_y + d) % ring) * 2 + core)

    partner = (tx, place_y * 2 + 1 - core)
    first_peer = (along_y, along_z)
    second_peer = (along_z, along_y)
    first_place = (place_y, place_z)
    second_place = (place_z, place_y)

    def toward(route):
        ex, ey = route
        return ((tx + ex + n_tx) % n_tx, (ty + ey + n_ty) % n_ty)

    def remote(src, dst, send, recv, device):
        return pltpu.make_async_remote_copy(
            src_ref=src, dst_ref=dst, send_sem=send, recv_sem=recv,
            device_id=device, device_id_type=MESH,
        )

    weight_copy = pltpu.make_async_copy(weight_hbm, weight, weight_sem)
    weight_copy.start()

    barrier = pltpu.get_barrier_semaphore()

    def greet(device):
        pl.semaphore_signal(barrier, inc=1, device_id=device, device_id_type=MESH)

    for route in ROUTES:
        greet(toward(route))
    greet(partner)
    for d in range(1, ring):
        greet(along_y(d))
        greet(along_z(d))
    for d in range(1, nx):
        greet(along_x(d))

    for slot in range(4):
        i, j = slot // 2, slot % 2
        active = (near_ref[13, slot] >= 0).astype(jnp.int32)
        row = (occ_ref[slot : slot + 1, :] * active).astype(F32)
        column = jnp.broadcast_to(row, (128, 128)).T
        occ_cells[4 * i : 4 * i + 4, 4 * j : 4 * j + 4] = column.reshape(4, 4, 8, 128)
        masked = feat_ref[slot].astype(F32) * column
        cells[1 + 4 * i : 5 + 4 * i, 1 + 4 * j : 5 + 4 * j] = masked.reshape(4, 4, 8, 128)

    def halo_copy(turn, index):
        count = 64 if index < 4 else 16
        return remote(
            halo_out.at[turn, index, 0:count], halo_in.at[turn, index, 0:count],
            halo_send.at[turn, index], halo_recv.at[turn, index], toward(ROUTES[index]),
        )

    def stage_halo(turn):
        for index, (ex, ey) in enumerate(ROUTES):
            block = cells[span_to_send(ex), span_to_send(ey)]
            if index < 4:
                halo_out[turn, index] = block.reshape(64, 128).astype(BF16)
            else:
                block = block.reshape(8, 128)
                halo_out[turn, index, 0:16] = jnp.concatenate([block, block], axis=0).astype(BF16)

    def send_halo(turn):
        for index in (4, 5, 6, 7, 0, 1, 2, 3):
            halo_copy(turn, index).start()

    def take_halo(turn):
        for index, (ex, ey) in enumerate(ROUTES):
            halo_copy(turn, index).wait_recv()
            from_x, from_y = tx - ex, ty - ey
            inside = (from_x >= 0) & (from_x < n_tx) & (from_y >= 0) & (from_y < n_ty)
            keep = inside.astype(jnp.int32).astype(F32)
            if index < 4:
                block = halo_in[turn, index].astype(F32) * keep
                shape = (1, 8, 8, 128) if ex else (8, 1, 8, 128)
            else:
                block = halo_in[turn, index, 0:16].astype(F32)[0:8] * keep
                shape = (1, 1, 8, 128)
            cells[span_received(ex), span_received(ey)] = block.reshape(shape)

    layer = lax.broadcasted_iota(jnp.int32, (80, 8, 128), 1)

    def fill_columns(target, flip):
        for dy in range(3):
            start = 2 - dy if flip else dy
            block = cells[:, start : start + 8].reshape(80, 8, 128)
            for dz in range(3):
                move = 1 - dz if flip else dz - 1
                if move > 0:
                    shifted = jnp.where(layer == 7, 0.0, pltpu.roll(block, 7, 1))
                elif move < 0:
                    shifted = jnp.where(layer == 0, 0.0, pltpu.roll(block, 1, 1))
                else:
                    shifted = block
                lane = 128 * (3 * dy + dz)
                target[:, lane : lane + 128] = shifted.reshape(640, 128).astype(BF16)

    stage_halo(0)
    pl.semaphore_wait(barrier, 9 + 2 * (ring - 1) + nx - 1)
    send_halo(0)

    teacher = jnp.exp(teacher_ref[...].astype(F32))
    target = teacher / jnp.sum(teacher, axis=0, keepdims=True)
    where = point_ref[...]
    spread = (
        (where // 256) * 256 + (where // 32) % 4 * 64
        + (where // 128) % 2 * 32 + where % 32
    )
    voxel = lax.broadcasted_iota(jnp.int32, (512, 1024), 0)
    hits = jnp.where(voxel == spread, 1.0, 0.0).astype(BF16)
    parts = jnp.concatenate([*split3(target), jnp.ones((16, 1024), BF16)], axis=0)
    sums = lax.dot_general(parts, hits, NT, preferred_element_type=F32)
    target_sum = sums[0:16] + (sums[16:32] + sums[32:48])
    points = sums[48:64]

    weight_copy.wait()
    for k in range(27):
        lane = 128 * (k % 9)
        weight_t[k // 9, :, lane : lane + 128] = weight[k]

    take_halo(0)
    fill_columns(columns, False)

    pre = jnp.zeros((512, 128), F32)
    for q in range(3):
        pre += jnp.dot(
            columns[64 * q : 64 * q + 512, :],
            weight[9 * q : 9 * q + 9].reshape(1152, 128),
            preferred_element_type=F32,
        )
    occupied = occ_cells[...].reshape(512, 128)
    logistic = 1.0 / (1.0 + jnp.exp(-pre))
    hidden = (pre * logistic * occupied).astype(BF16)
    slope = logistic * (1.0 + pre * (1.0 - logistic)) * occupied

    logits = lax.dot_general(head_ref[...], hidden, NT, preferred_element_type=F32)
    student = jnp.exp(logits)
    student = student / jnp.sum(student, axis=0, keepdims=True)
    slope_logits = jnp.where(points > 0.0, points * student - target_sum, 0.0)
    head3 = jnp.concatenate([head_ref[...]] * 3, axis=0)
    pieces = jnp.concatenate(split3(slope_logits), axis=0)
    dhidden = lax.dot_general(pieces, head3, TN, preferred_element_type=F32)
    dpre = (dhidden * slope).astype(BF16)

    cells[1:9, 1:9] = dpre.astype(F32).reshape(8, 8, 8, 128)
    stage_halo(1)
    send_halo(1)

    for q in range(3):
        term = lax.dot_general(
            columns[64 * q : 64 * q + 512, :], dpre, TN, preferred_element_type=F32
        )
        terms[9 * q : 9 * q + 9] = term.reshape(9, 128, 128)
    terms[27:28] = jnp.zeros((1, 128, 128), F32)

    def pair_copy(h, q):
        return remote(
            pair_out.at[h, q], pair_in.at[h, q],
            pair_send.at[h, q], pair_recv.at[h, q], partner,
        )

    def own_rows(which, q):
        return pl.ds(pl.multiple_of(which * 64 + q * rows, rows), rows)

    def pair_step(d, carry):
        for h in range(2):
            q = (first_place[h] + d) % ring
            value = terms[HALF * h : HALF * h + HALF, own_rows(1 - core, q), :]
            pair_out[h, q] = value.reshape(HALF * rows, 128).astype(BF16)
            pair_copy(h, q).start()
        return carry

    lax.fori_loop(1, ring + 1, pair_step, 0)

    take_halo(1)
    fill_columns(columns_g, True)

    def ring_copy(h, d):
        return remote(
            ring_out.at[h, d], ring_in.at[h, d],
            ring_send.at[h, d], ring_recv.at[h, d], first_peer[h](d),
        )

    def paired(h, q):
        pair_copy(h, q).wait_recv()
        own = terms[HALF * h : HALF * h + HALF, own_rows(core, q), :]
        return own + pair_in[h, q].astype(F32).reshape(HALF, rows, 128)

    def ring_step(d, carry):
        for h in range(2):
            q = (first_place[h] + d) % ring
            ring_out[h, d] = paired(h, q).reshape(HALF * rows, 128).astype(BF16)
            ring_copy(h, d).start()
        return carry

    lax.fori_loop(1, ring, ring_step, 0)
    for h in range(2):
        mid[h, 0:HALF] = paired(h, first_place[h])
        if per * ring > HALF:
            mid[h, HALF : per * ring] = jnp.zeros((per * ring - HALF, rows, 128), F32)

    back = jnp.zeros((512, 128), F32)
    for q in range(3):
        back += lax.dot_general(
            columns_g[64 * (2 - q) : 64 * (2 - q) + 512, :], weight_t[q], NT,
            preferred_element_type=F32,
        )
    back = (back * occ_cells[...].reshape(512, 128)).reshape(8, 8, 8, 128)
    for slot in range(4):
        i, j = slot // 2, slot % 2
        block = back[4 * i : 4 * i + 4, 4 * j : 4 * j + 4]
        grad_ref[slot] = block.reshape(128, 128).astype(BF16)

    def ring_sum(d, carry):
        for h in range(2):
            ring_copy(h, d).wait_recv()
            mid[h, 0:HALF] += ring_in[h, d].astype(F32).reshape(HALF, rows, 128)
        return carry

    lax.fori_loop(1, ring, ring_sum, 0)

    def mid_copy(h, d):
        p = (second_place[h] + d) % ring
        return remote(
            mid.at[h, pl.ds(p * per, per)], mid_in.at[h, d],
            mid_send.at[h, d], mid_recv.at[h, d], second_peer[h](d),
        )

    def each_peer(action):
        def step(d, carry):
            for h in range(2):
                action(h, d)
            return carry

        lax.fori_loop(1, ring, step, 0)

    each_peer(lambda h, d: mid_copy(h, d).start())
    for h in range(2):
        row_out[h] = mid[h, pl.ds(second_place[h] * per, per)]

    def mid_sum(h, d):
        mid_copy(h, d).wait_recv()
        row_out[h] += mid_in[h, d]

    each_peer(mid_sum)

    def row_copy(d):
        return remote(
            row_out, row_in.at[place_x], row_send.at[d], row_recv.at[d], along_x(d)
        )

    for d in range(1, nx):
        row_copy(d).start()
    row_in[place_x] = row_out[...]
    for d in range(1, nx):
        row_copy(d).wait_recv()
    total = row_in[0]
    for x in range(1, nx):
        total += row_in[x]
    for h in range(2):
        final = total[h].reshape(per * rows, 128).astype(BF16)
        last[h] = final
        full[core, h, first_place[h], second_place[h]] = final

    def thin_copy(h, d):
        return remote(
            last.at[h], full.at[core, h, first_place[h], second_place[h]],
            thin_send.at[h, d], thin_recv.at[h, d], second_peer[h](d),
        )

    each_peer(lambda h, d: thin_copy(h, d).start())
    each_peer(lambda h, d: thin_copy(h, d).wait_recv())

    def wide_copy(h, d):
        block = full.at[core, h, first_place[h], 0:used]
        return remote(
            block, block, wide_send.at[h, d], wide_recv.at[h, d], first_peer[h](d)
        )

    def core_copy(h, q):
        block = full.at[core, h, q, 0:used]
        return remote(block, block, core_send.at[h, q], core_recv.at[h, q], partner)

    each_peer(lambda h, d: wide_copy(h, d).start())
    for h in range(2):
        core_copy(h, first_place[h]).start()

    def pass_on(h, d):
        wide_copy(h, d).wait_recv()
        core_copy(h, (first_place[h] + ring - d) % ring).start()

    each_peer(pass_on)

    def collect(q, squares):
        for h in range(2):
            core_copy(h, q).wait_recv()
            for side in range(2):
                block = full[side, h, q, 0:used].astype(F32).reshape(used * per, rows, 128)
                count = HALF if h == 0 else 27 - HALF
                block = block[0:count]
                sum_ref[HALF * h : HALF * h + count, own_rows(side, q), :] = block
                squares = squares + jnp.sum((block * block).reshape(-1, 8, 128), axis=0)
        return squares

    squares = lax.fori_loop(0, ring, collect, jnp.zeros((8, 128), F32))
    mean = jnp.full((8, 128), jnp.sum(squares) / (27 * 128 * 128), F32)
    norm_ref[...] = 1.0 / jnp.sqrt(mean + 1e-06)

    for turn in range(2):
        for index in range(8):
            halo_copy(turn, index).wait_send()

    def sent(h, d):
        ring_copy(h, d).wait_send()
        mid_copy(h, d).wait_send()
        thin_copy(h, d).wait_send()
        wide_copy(h, d).wait_send()

    each_peer(sent)
    for d in range(1, nx):
        row_copy(d).wait_send()

    def sent_to_partner(q, carry):
        for h in range(2):
            pair_copy(h, q).wait_send()
            core_copy(h, q).wait_send()
        return carry

    lax.fori_loop(0, ring, sent_to_partner, 0)


def on_device(sizes, features, occupancy, neighbors, point_voxel, conv_weight, head_weight, teacher):
    nx, ring, per, used = sizes
    rows = 64 // ring
    dma = pltpu.SemaphoreType.DMA
    vmem = pl.BlockSpec(memory_space=pltpu.VMEM)
    grad, summed, norm = pl.pallas_call(
        functools.partial(kernel, sizes),
        out_shape=(
            jax.ShapeDtypeStruct((4, 128, 128), BF16),
            jax.ShapeDtypeStruct((27, 128, 128), F32),
            jax.ShapeDtypeStruct((8, 128), F32),
        ),
        in_specs=[
            pl.BlockSpec(memory_space=pltpu.SMEM),
            vmem, vmem, vmem,
            pl.BlockSpec(memory_space=pl.ANY),
            vmem, vmem,
        ],
        out_specs=(vmem, vmem, vmem),
        scratch_shapes=[
            pltpu.VMEM((10, 10, 8, 128), F32),
            pltpu.VMEM((8, 8, 8, 128), F32),
            pltpu.VMEM((640, 1152), BF16),
            pltpu.VMEM((640, 1152), BF16),
            pltpu.VMEM((27, 128, 128), BF16),
            pltpu.VMEM((3, 128, 1152), BF16),
            pltpu.VMEM((2, 8, 64, 128), BF16),
            pltpu.VMEM((2, 8, 64, 128), BF16),
            pltpu.VMEM((2 * HALF, 128, 128), F32),
            pltpu.VMEM((2, ring, HALF * rows, 128), BF16),
            pltpu.VMEM((2, ring, HALF * rows, 128), BF16),
            pltpu.VMEM((2, ring, HALF * rows, 128), BF16),
            pltpu.VMEM((2, ring, HALF * rows, 128), BF16),
            pltpu.VMEM((2, per * ring, rows, 128), F32),
            pltpu.VMEM((2, ring, per, rows, 128), F32),
            pltpu.VMEM((2, per, rows, 128), F32),
            pltpu.VMEM((nx, 2, per, rows, 128), F32),
            pltpu.VMEM((2, per * rows, 128), BF16),
            pltpu.VMEM((2, 2, ring, ring, per * rows, 128), BF16),
            dma,
            dma((2, 8)), dma((2, 8)),
            dma((2, ring)), dma((2, ring)),
            dma((2, ring)), dma((2, ring)),
            dma((2, ring)), dma((2, ring)),
            dma((nx,)), dma((nx,)),
            dma((2, ring)), dma((2, ring)),
            dma((2, ring)), dma((2, ring)),
            dma((2, ring)), dma((2, ring)),
        ],
        compiler_params=pltpu.CompilerParams(
            collective_id=0, has_side_effects=True, vmem_limit_bytes=48 * 1024 * 1024
        ),
    )(
        neighbors, occupancy, features, point_voxel.reshape(1, -1), conv_weight,
        head_weight, teacher,
    )
    return grad, summed * norm[0, 0]


def solution(mesh):
    ring = mesh.shape["ty"] // 2
    nx = mesh.shape["tx"] // ring
    per = -(-HALF // ring)
    used = -(-HALF // per)
    in_specs = (
        P(("tx", "ty"), None, None),
        P(("tx", "ty"), None),
        P(None, ("tx", "ty")),
        P(("tx", "ty")),
        P(),
        P(),
        P(None, ("tx", "ty")),
    )
    out_specs = (P(("tx", "ty"), None, None), P())
    return jax.shard_map(
        functools.partial(on_device, (nx, ring, per, used)),
        mesh=mesh, in_specs=in_specs, out_specs=out_specs, check_vma=False,
    )
```

```python
import functools

import jax
import jax.numpy as jnp
from jax import lax
from jax.experimental import pallas as pl
from jax.experimental.pallas import tpu as pltpu
from jax.sharding import PartitionSpec as P

F32 = jnp.float32
BF16 = jnp.bfloat16
MESH = pl.DeviceIdType.MESH
ROUTES = ((-1, 0), (1, 0), (0, -1), (0, 1), (-1, -1), (-1, 1), (1, -1), (1, 1))
TN = (((0,), (0,)), ((), ()))
NT = (((1,), (1,)), ((), ()))
PARTS = ((0, 8, "yzx"), (8, 8, "zyx"), (16, 11, "xyz"))


def far_first(n):
    return sorted(range(1, n), key=lambda d: (-min(d, n - d), d))


def near_first(n):
    return sorted(range(n), key=lambda d: (min(d, n - d), d))


def slot_groups(n):
    if n < 4:
        return [(s, s + 1) for s in range(n)]
    return [(0, 3), (3, n - 1), (n - 1, n)]


class Part:
    def __init__(self, place, first, count, axes, size):
        self.index = place
        self.first, self.count = first, count
        self.a1, self.a2, self.a3 = axes
        self.n1, self.n2, self.n3 = (size[axis] for axis in axes)
        self.rows = 64 // self.n1
        self.tiles = count * self.rows // 8
        self.per = -(-self.tiles // self.n2)
        self.near2 = near_first(self.n2)
        self.groups = slot_groups(self.n2)


def make_parts(nx, ring):
    size = {"x": nx, "y": ring, "z": ring}
    return [Part(i, *spec, size) for i, spec in enumerate(PARTS)]


def scratch_of(part):
    dma = pltpu.SemaphoreType.DMA
    wide = pltpu.VMEM((part.n1, part.tiles * 8, 128), BF16)
    return {
        "pair_out": wide, "pair_in": wide, "ring_out": wide, "ring_in": wide,
        "mid": pltpu.VMEM((part.n2 * part.per, 8, 128), F32),
        "mid_in": pltpu.VMEM((part.n2, part.per, 8, 128), F32),
        "row_out": pltpu.VMEM((part.per, 8, 128), F32),
        "row_in": pltpu.VMEM((part.n3, part.per, 8, 128), F32),
        "full": pltpu.VMEM((2, part.n1, part.n2, part.per * 8, 128), BF16),
        "tiles": pltpu.VMEM((part.n2 * part.per, 8, 128), F32),
        "pair_send": dma((part.n1,)), "pair_recv": dma((part.n1,)),
        "ring_send": dma((part.n1,)), "ring_recv": dma((part.n1,)),
        "mid_send": dma((part.n2,)), "mid_recv": dma((part.n2,)),
        "row_send": dma((part.n3,)), "row_recv": dma((part.n3,)),
        "thin_send": dma((part.n2,)), "thin_recv": dma((part.n2,)),
        "wide_send": dma((len(part.groups), part.n1)),
        "wide_recv": dma((len(part.groups), part.n1)),
        "core_send": dma((len(part.groups), part.n1)),
        "core_recv": dma((len(part.groups), part.n1)),
    }


def span_to_send(step):
    if step < 0:
        return slice(1, 2)
    if step > 0:
        return slice(8, 9)
    return slice(1, 9)


def span_received(step):
    if step < 0:
        return slice(9, 10)
    if step > 0:
        return slice(0, 1)
    return slice(1, 9)


def split3(value):
    one = value.astype(BF16)
    rest = value - one.astype(F32)
    two = rest.astype(BF16)
    three = (rest - two.astype(F32)).astype(BF16)
    return one, two, three


def kernel(sizes, names, *refs):
    nx, ring = sizes
    parts = make_parts(nx, ring)
    in_hbm, (grad_ref, sum_ref, norm_ref) = refs[:7], refs[7:10]
    (
        near_ref, occ_ref, feat_ref, point_ref, weight, head_ref, teacher_ref, input_sem,
        cells, occ_cells, columns, columns_g, weight_t, halo_out, halo_in, terms,
        halo_send, halo_recv,
    ) = refs[10:28]
    rest = iter(refs[28:])
    for part in parts:
        for name in names:
            setattr(part, name, next(rest))

    n_tx, n_ty = nx * ring, 2 * ring
    tx = lax.axis_index("tx")
    ty = lax.axis_index("ty")
    core = ty % 2
    place = {"x": tx // ring, "z": tx % ring, "y": ty // 2}
    extent = {"x": nx, "y": ring, "z": ring}

    def along(axis, d):
        if axis == "x":
            return (((place["x"] + d) % nx) * ring + place["z"], ty)
        if axis == "z":
            return (place["x"] * ring + (place["z"] + d) % ring, ty)
        return (tx, ((place["y"] + d) % ring) * 2 + core)

    peers = {axis: [along(axis, d) for d in range(extent[axis])] for axis in "xyz"}
    partner = (tx, place["y"] * 2 + 1 - core)

    def toward(route):
        ex, ey = route
        return ((tx + ex + n_tx) % n_tx, (ty + ey + n_ty) % n_ty)

    def remote(src, dst, send, recv, device):
        return pltpu.make_async_remote_copy(
            src_ref=src, dst_ref=dst, send_sem=send, recv_sem=recv,
            device_id=device, device_id_type=MESH,
        )

    barrier = pltpu.get_barrier_semaphore()

    def greet(device):
        pl.semaphore_signal(barrier, inc=1, device_id=device, device_id_type=MESH)

    for route in ROUTES:
        greet(toward(route))
    held = (near_ref, occ_ref, feat_ref, point_ref, weight, head_ref, teacher_ref)
    inputs = [
        pltpu.make_async_copy(src, dst, input_sem.at[i])
        for i, (src, dst) in enumerate(zip(in_hbm, held))
    ]
    for i in (0, 1, 2, 3, 6, 5, 4):
        inputs[i].start()
    greet(partner)
    for axis in "yzx":
        for d in far_first(extent[axis]):
            greet(peers[axis][d])

    for i in (0, 1, 2):
        inputs[i].wait()
    active = (near_ref[:, 13:14] >= 0).astype(jnp.int32)
    occupancy = (occ_ref[...] * active).astype(F32)
    for slot in range(4):
        i, j = slot // 2, slot % 2
        column = jnp.broadcast_to(occupancy[slot : slot + 1, :], (128, 128)).T
        occ_cells[4 * i : 4 * i + 4, 4 * j : 4 * j + 4] = column.reshape(4, 4, 8, 128)
        masked = feat_ref[slot].astype(F32) * column
        cells[1 + 4 * i : 5 + 4 * i, 1 + 4 * j : 5 + 4 * j] = masked.reshape(4, 4, 8, 128)

    def halo_copy(turn, index):
        count = 64 if index < 4 else 16
        return remote(
            halo_out.at[turn, index, 0:count], halo_in.at[turn, index, 0:count],
            halo_send.at[turn, index], halo_recv.at[turn, index], toward(ROUTES[index]),
        )

    def stage_halo(turn):
        for index, (ex, ey) in enumerate(ROUTES):
            block = cells[span_to_send(ex), span_to_send(ey)]
            if index < 4:
                halo_out[turn, index] = block.reshape(64, 128).astype(BF16)
            else:
                block = block.reshape(8, 128)
                halo_out[turn, index, 0:16] = jnp.concatenate([block, block], axis=0).astype(BF16)

    def send_halo(turn):
        for index in (4, 5, 6, 7, 0, 1, 2, 3):
            halo_copy(turn, index).start()

    def take_halo(turn):
        for index, (ex, ey) in enumerate(ROUTES):
            halo_copy(turn, index).wait_recv()
            from_x, from_y = tx - ex, ty - ey
            inside = (from_x >= 0) & (from_x < n_tx) & (from_y >= 0) & (from_y < n_ty)
            keep = inside.astype(jnp.int32).astype(F32)
            if index < 4:
                block = halo_in[turn, index].astype(F32) * keep
                shape = (1, 8, 8, 128) if ex else (8, 1, 8, 128)
            else:
                block = halo_in[turn, index, 0:16].astype(F32)[0:8] * keep
                shape = (1, 1, 8, 128)
            cells[span_received(ex), span_received(ey)] = block.reshape(shape)

    layer = lax.broadcasted_iota(jnp.int32, (80, 8, 128), 1)

    def fill_columns(target, flip):
        for dy in range(3):
            start = 2 - dy if flip else dy
            block = cells[:, start : start + 8].reshape(80, 8, 128)
            for dz in range(3):
                move = 1 - dz if flip else dz - 1
                if move > 0:
                    shifted = jnp.where(layer == 7, 0.0, pltpu.roll(block, 7, 1))
                elif move < 0:
                    shifted = jnp.where(layer == 0, 0.0, pltpu.roll(block, 1, 1))
                else:
                    shifted = block
                lane = 128 * (3 * dy + dz)
                target[:, lane : lane + 128] = shifted.reshape(640, 128).astype(BF16)

    stage_halo(0)
    pl.semaphore_wait(barrier, 9 + 2 * (ring - 1) + nx - 1)
    send_halo(0)

    for i in (3, 6, 5, 4):
        inputs[i].wait()
    teacher = jnp.exp(teacher_ref[...].astype(F32))
    target = teacher / jnp.sum(teacher, axis=0, keepdims=True)
    where = point_ref[...]
    spread = (
        (where // 256) * 256 + (where // 32) % 4 * 64
        + (where // 128) % 2 * 32 + where % 32
    )
    voxel = lax.broadcasted_iota(jnp.int32, (512, 1024), 0)
    hits = jnp.where(voxel == spread, 1.0, 0.0).astype(BF16)
    stack = jnp.concatenate([*split3(target), jnp.ones((16, 1024), BF16)], axis=0)
    sums = lax.dot_general(stack, hits, NT, preferred_element_type=F32)
    target_sum = sums[0:16] + (sums[16:32] + sums[32:48])
    points = sums[48:64]

    for k in range(27):
        lane = 128 * (k % 9)
        weight_t[k // 9, :, lane : lane + 128] = weight[k]

    take_halo(0)
    fill_columns(columns, False)

    pre = jnp.zeros((512, 128), F32)
    for q in range(3):
        pre += jnp.dot(
            columns[64 * q : 64 * q + 512, :],
            weight[9 * q : 9 * q + 9].reshape(1152, 128),
            preferred_element_type=F32,
        )
    occupied = occ_cells[...].reshape(512, 128)
    logistic = 1.0 / (1.0 + jnp.exp(-pre))
    hidden = (pre * logistic * occupied).astype(BF16)
    slope = logistic * (1.0 + pre * (1.0 - logistic)) * occupied

    logits = lax.dot_general(head_ref[...], hidden, NT, preferred_element_type=F32)
    student = jnp.exp(logits)
    student = student / jnp.sum(student, axis=0, keepdims=True)
    slope_logits = jnp.where(points > 0.0, points * student - target_sum, 0.0)
    head3 = jnp.concatenate([head_ref[...]] * 3, axis=0)
    pieces = jnp.concatenate(split3(slope_logits), axis=0)
    dhidden = lax.dot_general(pieces, head3, TN, preferred_element_type=F32)
    dpre = (dhidden * slope).astype(BF16)

    cells[1:9, 1:9] = dpre.astype(F32).reshape(8, 8, 8, 128)
    stage_halo(1)
    send_halo(1)

    def own_rows(part, side, q):
        return pl.ds(pl.multiple_of(side * 64 + q * part.rows, part.rows), part.rows)

    def pair_copy(part, q):
        return remote(
            part.pair_out.at[q], part.pair_in.at[q],
            part.pair_send.at[q], part.pair_recv.at[q], partner,
        )

    def block_at(part, d):
        return (place[part.a1] + d) % part.n1

    def my_term(part, side, q):
        block = terms[part.first : part.first + part.count, own_rows(part, side, q), :]
        return block.reshape(part.tiles * 8, 128)

    for turn, part in enumerate(parts):
        term = lax.dot_general(
            columns[64 * turn : 64 * turn + 512, :], dpre, TN, preferred_element_type=F32
        )
        terms[9 * turn : 9 * turn + 9] = term.reshape(9, 128, 128)
        for d in far_first(part.n1) + [0]:
            q = block_at(part, d)
            part.pair_out[q] = my_term(part, 1 - core, q).astype(BF16)
            pair_copy(part, q).start()

    def ring_copy(part, d):
        return remote(
            part.ring_out.at[d], part.ring_in.at[d],
            part.ring_send.at[d], part.ring_recv.at[d], peers[part.a1][d],
        )

    def paired(part, q):
        pair_copy(part, q).wait_recv()
        return my_term(part, core, q) + part.pair_in[q].astype(F32)

    orders = {part.index: far_first(part.n1) for part in parts}
    for turn in range(max(len(order) for order in orders.values())):
        for part in parts:
            if turn < len(orders[part.index]):
                d = orders[part.index][turn]
                part.ring_out[d] = paired(part, block_at(part, d)).astype(BF16)
                ring_copy(part, d).start()
    for part in parts:
        own = paired(part, block_at(part, 0))
        part.mid[0 : part.tiles] = own.reshape(part.tiles, 8, 128)
        spare = part.per * part.n2 - part.tiles
        if spare:
            part.mid[part.tiles :] = jnp.zeros((spare, 8, 128), F32)

    take_halo(1)
    fill_columns(columns_g, True)
    back = jnp.zeros((512, 128), F32)
    for q in range(3):
        back += lax.dot_general(
            columns_g[64 * (2 - q) : 64 * (2 - q) + 512, :], weight_t[q], NT,
            preferred_element_type=F32,
        )
    back = (back * occ_cells[...].reshape(512, 128)).reshape(8, 8, 8, 128)
    for slot in range(4):
        i, j = slot // 2, slot % 2
        block = back[4 * i : 4 * i + 4, 4 * j : 4 * j + 4]
        grad_ref[slot] = block.reshape(128, 128).astype(BF16)

    def mid_copy(part, d):
        p = (place[part.a2] + d) % part.n2
        return remote(
            part.mid.at[pl.ds(p * part.per, part.per)], part.mid_in.at[d],
            part.mid_send.at[d], part.mid_recv.at[d], peers[part.a2][d],
        )

    last_first = (parts[2], parts[0], parts[1])
    for part in last_first:
        block = part.mid[0 : part.tiles]
        for d in reversed(far_first(part.n1)):
            ring_copy(part, d).wait_recv()
            block = block + part.ring_in[d].astype(F32).reshape(part.tiles, 8, 128)
        part.mid[0 : part.tiles] = block
        for d in far_first(part.n2):
            mid_copy(part, d).start()

    def row_copy(part, d):
        return remote(
            part.row_out, part.row_in.at[place[part.a3]],
            part.row_send.at[d], part.row_recv.at[d], peers[part.a3][d],
        )

    for part in last_first:
        block = part.mid[pl.ds(place[part.a2] * part.per, part.per)]
        for d in reversed(far_first(part.n2)):
            mid_copy(part, d).wait_recv()
            block = block + part.mid_in[d]
        part.row_out[...] = block
        for d in far_first(part.n3):
            row_copy(part, d).start()
        part.row_in[place[part.a3]] = block

    def thin_copy(part, slot):
        home = part.full.at[core, place[part.a1]]
        return remote(
            home.at[0], home.at[slot],
            part.thin_send.at[slot], part.thin_recv.at[slot],
            peers[part.a2][part.near2[slot]],
        )

    def wide_copy(part, group, d):
        start, stop = part.groups[group]
        block = part.full.at[core, place[part.a1], start:stop]
        return remote(
            block, block, part.wide_send.at[group, d], part.wide_recv.at[group, d],
            peers[part.a1][d],
        )

    def core_copy(part, group, q):
        start, stop = part.groups[group]
        block = part.full.at[core, q, start:stop]
        return remote(
            block, block, part.core_send.at[group, q], part.core_recv.at[group, q], partner
        )

    for part in (parts[0], parts[1], parts[2]):
        for d in reversed(far_first(part.n3)):
            row_copy(part, d).wait_recv()
        total = part.row_in[0]
        for x in range(1, part.n3):
            total = total + part.row_in[x]
        part.full[core, place[part.a1], 0] = total.reshape(part.per * 8, 128).astype(BF16)
        for slot in reversed(range(1, part.n2)):
            thin_copy(part, slot).start()

    rounds = max(len(part.groups) for part in parts)
    for group in range(rounds):
        for part in parts:
            start, stop = part.groups[group]
            for slot in range(max(start, 1), stop):
                thin_copy(part, slot).wait_recv()
            for d in far_first(part.n1):
                wide_copy(part, group, d).start()
            core_copy(part, group, block_at(part, 0)).start()
    for group in range(rounds):
        for part in parts:
            for d in reversed(far_first(part.n1)):
                wide_copy(part, group, d).wait_recv()
                core_copy(part, group, block_at(part, part.n1 - d)).start()

    squares = jnp.zeros((8, 128), F32)
    for part in parts:
        where = [
            (place[part.a2] + part.n2 - part.near2[slot]) % part.n2 for slot in range(part.n2)
        ]
        for step in range(2 * part.n1):
            side, q = step // part.n1, step % part.n1
            if side == 0:
                side = core
            else:
                side = 1 - core
                for group in range(len(part.groups)):
                    core_copy(part, group, q).wait_recv()
            for slot in range(part.n2):
                piece = part.full[side, q, slot].astype(F32).reshape(part.per, 8, 128)
                part.tiles_ref[pl.ds(where[slot] * part.per, part.per)] = piece
            block = part.tiles_ref[0 : part.tiles]
            squares = squares + jnp.sum(block * block, axis=0)
            sum_ref[part.first : part.first + part.count, own_rows(part, side, q), :] = (
                block.reshape(part.count, part.rows, 128)
            )
    mean = jnp.full((8, 128), jnp.sum(squares) / (27 * 128 * 128), F32)
    norm_ref[...] = 1.0 / jnp.sqrt(mean + 1e-06)

    for turn in range(2):
        for index in range(8):
            halo_copy(turn, index).wait_send()
    for part in parts:
        for q in range(part.n1):
            pair_copy(part, q).wait_send()
            for group in range(len(part.groups)):
                core_copy(part, group, q).wait_send()
        for d in range(1, part.n1):
            ring_copy(part, d).wait_send()
            for group in range(len(part.groups)):
                wide_copy(part, group, d).wait_send()
        for d in range(1, part.n2):
            mid_copy(part, d).wait_send()
            thin_copy(part, d).wait_send()
        for d in range(1, part.n3):
            row_copy(part, d).wait_send()


def finish_kernel(grad_ref, sum_ref, norm_ref, grad_out, sum_out, staged, sems):
    grad_copy = pltpu.make_async_copy(grad_ref, grad_out, sems.at[9])
    grad_copy.start()
    norm = norm_ref[...].reshape(1, 1, 8, 128)
    copies = []
    for step in range(9):
        span = slice(3 * step, 3 * step + 3)
        block = sum_ref[span].reshape(3, 16, 8, 128) * norm
        staged[span] = block.reshape(3, 128, 128)
        copies.append(pltpu.make_async_copy(staged.at[span], sum_out.at[span], sems.at[step]))
        copies[-1].start()
    for copy in copies:
        copy.wait()
    grad_copy.wait()


def on_device(sizes, features, occupancy, neighbors, point_voxel, conv_weight, head_weight, teacher):
    nx, ring = sizes
    parts = make_parts(nx, ring)
    dma = pltpu.SemaphoreType.DMA
    vmem = pl.BlockSpec(memory_space=pltpu.VMEM)
    hbm = pl.BlockSpec(memory_space=pltpu.HBM)
    args = (
        neighbors.T, occupancy, features, point_voxel.reshape(1, -1), conv_weight,
        head_weight, teacher,
    )
    own = [scratch_of(part) for part in parts]
    names = ["tiles_ref" if name == "tiles" else name for name in own[0]]
    grad, summed, norm = pl.pallas_call(
        functools.partial(kernel, sizes, names),
        out_shape=(
            jax.ShapeDtypeStruct((4, 128, 128), BF16),
            jax.ShapeDtypeStruct((27, 128, 128), F32),
            jax.ShapeDtypeStruct((8, 128), F32),
        ),
        in_specs=[hbm] * 7,
        out_specs=(vmem, vmem, vmem),
        scratch_shapes=[
            *(pltpu.VMEM(arg.shape, arg.dtype) for arg in args),
            dma((7,)),
            pltpu.VMEM((10, 10, 8, 128), F32),
            pltpu.VMEM((8, 8, 8, 128), F32),
            pltpu.VMEM((640, 1152), BF16),
            pltpu.VMEM((640, 1152), BF16),
            pltpu.VMEM((3, 128, 1152), BF16),
            pltpu.VMEM((2, 8, 64, 128), BF16),
            pltpu.VMEM((2, 8, 64, 128), BF16),
            pltpu.VMEM((27, 128, 128), F32),
            dma((2, 8)), dma((2, 8)),
            *(shape for table in own for shape in table.values()),
        ],
        compiler_params=pltpu.CompilerParams(
            collective_id=0, has_side_effects=True, vmem_limit_bytes=48 * 1024 * 1024
        ),
    )(*(pltpu.with_memory_space_constraint(arg, pltpu.HBM) for arg in args))
    return pl.pallas_call(
        finish_kernel,
        out_shape=(
            jax.ShapeDtypeStruct((4, 128, 128), BF16),
            jax.ShapeDtypeStruct((27, 128, 128), F32),
        ),
        in_specs=[vmem, vmem, vmem],
        out_specs=(hbm, hbm),
        scratch_shapes=[pltpu.VMEM((27, 128, 128), F32), dma((10,))],
        compiler_params=pltpu.CompilerParams(vmem_limit_bytes=16 * 1024 * 1024),
    )(grad, summed, norm)


def solution(mesh):
    ring = mesh.shape["ty"] // 2
    nx = mesh.shape["tx"] // ring
    in_specs = (
        P(("tx", "ty"), None, None),
        P(("tx", "ty"), None),
        P(None, ("tx", "ty")),
        P(("tx", "ty")),
        P(),
        P(),
        P(None, ("tx", "ty")),
    )
    out_specs = (P(("tx", "ty"), None, None), P())
    return jax.shard_map(
        functools.partial(on_device, (nx, ring)),
        mesh=mesh, in_specs=in_specs, out_specs=out_specs, check_vma=False,
    )
```

```python
import functools

import jax
import jax.numpy as jnp
from jax import lax
from jax.experimental import pallas as pl
from jax.experimental.pallas import tpu as pltpu
from jax.sharding import PartitionSpec as P

F32 = jnp.float32
BF16 = jnp.bfloat16
MESH = pl.DeviceIdType.MESH
ROUTES = ((-1, 0), (1, 0), (0, -1), (0, 1), (-1, -1), (-1, 1), (1, -1), (1, 1))
TN = (((0,), (0,)), ((), ()))
NT = (((1,), (1,)), ((), ()))
PARTS = ((0, 8, "yzx"), (8, 8, "zyx"), (16, 11, "xyz"))


def far_first(n):
    return sorted(range(1, n), key=lambda d: (-min(d, n - d), d))


def near_first(n):
    return sorted(range(n), key=lambda d: (min(d, n - d), d))


def runs(n, *cuts):
    edges = sorted({0, n, *(cut for cut in cuts if cut < n)})
    return list(zip(edges, edges[1:]))


class Part:
    def __init__(self, place, first, count, axes, size):
        self.index = place
        self.first, self.count = first, count
        self.a1, self.a2, self.a3 = axes
        self.n1, self.n2, self.n3 = (size[axis] for axis in axes)
        self.rows = 64 // self.n1
        self.tiles = count * self.rows // 8
        self.per = -(-self.tiles // self.n2)
        self.far1 = far_first(self.n1) + [0]
        self.near1 = near_first(self.n1)
        self.near2 = near_first(self.n2)
        self.pair_runs = runs(self.n1)
        self.core_runs = runs(self.n1)


def make_parts(nx, ring):
    size = {"x": nx, "y": ring, "z": ring}
    return [Part(i, *spec, size) for i, spec in enumerate(PARTS)]


def scratch_of(part):
    dma = pltpu.SemaphoreType.DMA
    wide = pltpu.VMEM((part.n1, part.tiles * 8, 128), BF16)
    return {
        "pair_out": wide, "pair_in": wide, "ring_out": wide, "ring_in": wide,
        "mid": pltpu.VMEM((part.n2 * part.per, 8, 128), F32),
        "mid_in": pltpu.VMEM((part.n2, part.per, 8, 128), F32),
        "row_out": pltpu.VMEM((part.per * 8, 128), F32),
        "row_in": pltpu.VMEM((part.n3, part.per * 8, 128), F32),
        "full": pltpu.VMEM((2, part.n1, part.n2, part.per * 8, 128), BF16),
        "tiles": pltpu.VMEM((part.n2 * part.per, 8, 128), F32),
        "squares": pltpu.VMEM((2, part.n1, 8, 128), F32),
        "pair_send": dma((len(part.pair_runs),)), "pair_recv": dma((len(part.pair_runs),)),
        "ring_send": dma((part.n1,)), "ring_recv": dma((part.n1,)),
        "mid_send": dma((part.n2,)), "mid_recv": dma((part.n2,)),
        "row_send": dma((part.n3,)), "row_recv": dma((part.n3,)),
        "thin_send": dma((part.n2,)), "thin_recv": dma((part.n2,)),
        "wide_send": dma((part.n1,)), "wide_recv": dma((part.n1,)),
        "core_send": dma((len(part.core_runs),)), "core_recv": dma((len(part.core_runs),)),
    }


def span_to_send(step):
    if step < 0:
        return slice(1, 2)
    if step > 0:
        return slice(8, 9)
    return slice(1, 9)


def span_received(step):
    if step < 0:
        return slice(9, 10)
    if step > 0:
        return slice(0, 1)
    return slice(1, 9)


def split3(value):
    one = value.astype(BF16)
    rest = value - one.astype(F32)
    two = rest.astype(BF16)
    three = (rest - two.astype(F32)).astype(BF16)
    return one, two, three


def kernel(sizes, names, *refs):
    nx, ring = sizes
    parts = make_parts(nx, ring)
    in_hbm, (grad_ref, sum_ref, norm_ref) = refs[:7], refs[7:10]
    (
        near_ref, occ_ref, feat_ref, point_ref, weight, head_ref, teacher_ref, input_sem,
        cells, occ_cells, columns, columns_g, weight_t, halo_out, halo_in, terms,
        halo_send, halo_recv, word_sem,
    ) = refs[10:29]
    rest = iter(refs[29:])
    for part in parts:
        for name in names:
            setattr(part, name, next(rest))

    n_tx, n_ty = nx * ring, 2 * ring
    tx = lax.axis_index("tx")
    ty = lax.axis_index("ty")
    core = ty % 2
    place = {"x": tx // ring, "z": tx % ring, "y": ty // 2}
    extent = {"x": nx, "y": ring, "z": ring}

    def along(axis, d):
        if axis == "x":
            return (((place["x"] + d) % nx) * ring + place["z"], ty)
        if axis == "z":
            return (place["x"] * ring + (place["z"] + d) % ring, ty)
        return (tx, ((place["y"] + d) % ring) * 2 + core)

    peers = {axis: [along(axis, d) for d in range(extent[axis])] for axis in "xyz"}
    partner = (tx, place["y"] * 2 + 1 - core)

    def toward(route):
        ex, ey = route
        return ((tx + ex + n_tx) % n_tx, (ty + ey + n_ty) % n_ty)

    def remote(src, dst, send, recv, device):
        return pltpu.make_async_remote_copy(
            src_ref=src, dst_ref=dst, send_sem=send, recv_sem=recv,
            device_id=device, device_id_type=MESH,
        )

    barrier = pltpu.get_barrier_semaphore()

    def greet(device):
        pl.semaphore_signal(barrier, inc=1, device_id=device, device_id_type=MESH)

    def on_map(x, y):
        return (x >= 0) & (x < n_tx) & (y >= 0) & (y < n_ty)

    leads = [on_map(tx + ex, ty + ey) for ex, ey in ROUTES]
    comes = [on_map(tx - ex, ty - ey) for ex, ey in ROUTES]
    greeted = 0
    for route, valid in zip(ROUTES, leads):
        pl.when(valid)(functools.partial(greet, toward(route)))
        greeted = greeted + valid.astype(jnp.int32)
    held = (near_ref, occ_ref, feat_ref, point_ref, weight, head_ref, teacher_ref)
    inputs = [
        pltpu.make_async_copy(src, dst, input_sem.at[i])
        for i, (src, dst) in enumerate(zip(in_hbm, held))
    ]
    for i in (0, 1, 2, 3, 6, 5, 4):
        inputs[i].start()
    others = [peers[axis][d] for axis in "yz" for d in (1, ring - 1)]
    others += [partner] + [peers["x"][d] for d in far_first(nx)]
    for device in others:
        greet(device)

    def pass_word(steps):
        for i, axis in enumerate("yz"):
            for way, d in enumerate((1, ring - 1)):
                pl.semaphore_signal(
                    word_sem.at[i, way, steps], inc=1, device_id=peers[axis][d],
                    device_id_type=MESH,
                )

    def await_word(steps):
        for i in range(2):
            for way in range(2):
                pl.semaphore_wait(word_sem.at[i, way, steps], 1)

    for i in (0, 1, 2):
        inputs[i].wait()
    active = (near_ref[:, 13:14] >= 0).astype(jnp.int32)
    occupancy = (occ_ref[...] * active).astype(F32)
    for slot in range(4):
        i, j = slot // 2, slot % 2
        column = jnp.broadcast_to(occupancy[slot : slot + 1, :], (128, 128)).T
        occ_cells[4 * i : 4 * i + 4, 4 * j : 4 * j + 4] = column.reshape(4, 4, 8, 128)
        masked = feat_ref[slot].astype(F32) * column
        cells[1 + 4 * i : 5 + 4 * i, 1 + 4 * j : 5 + 4 * j] = masked.reshape(4, 4, 8, 128)

    def halo_copy(turn, index):
        count = 64 if index < 4 else 16
        return remote(
            halo_out.at[turn, index, 0:count], halo_in.at[turn, index, 0:count],
            halo_send.at[turn, index], halo_recv.at[turn, index], toward(ROUTES[index]),
        )

    def stage_halo(turn):
        for index, (ex, ey) in enumerate(ROUTES):
            block = cells[span_to_send(ex), span_to_send(ey)]
            if index < 4:
                halo_out[turn, index] = block.reshape(64, 128).astype(BF16)
            else:
                block = block.reshape(8, 128)
                halo_out[turn, index, 0:16] = jnp.concatenate([block, block], axis=0).astype(BF16)

    def send_halo(turn):
        for index in (4, 5, 6, 7, 0, 1, 2, 3):
            pl.when(leads[index])(halo_copy(turn, index).start)

    def take_halo(turn):
        for index, (ex, ey) in enumerate(ROUTES):
            pl.when(comes[index])(halo_copy(turn, index).wait_recv)
            if index < 4:
                block = halo_in[turn, index].astype(F32)
                shape = (1, 8, 8, 128) if ex else (8, 1, 8, 128)
            else:
                block = halo_in[turn, index, 0:16].astype(F32)[0:8]
                shape = (1, 1, 8, 128)
            block = jnp.where(comes[index], block, 0.0)
            cells[span_received(ex), span_received(ey)] = block.reshape(shape)

    layer = lax.broadcasted_iota(jnp.int32, (80, 8, 128), 1)

    def fill_columns(target, flip):
        for dy in range(3):
            start = 2 - dy if flip else dy
            block = cells[:, start : start + 8].reshape(80, 8, 128)
            for dz in range(3):
                move = 1 - dz if flip else dz - 1
                if move > 0:
                    shifted = jnp.where(layer == 7, 0.0, pltpu.roll(block, 7, 1))
                elif move < 0:
                    shifted = jnp.where(layer == 0, 0.0, pltpu.roll(block, 1, 1))
                else:
                    shifted = block
                lane = 128 * (3 * dy + dz)
                target[:, lane : lane + 128] = shifted.reshape(640, 128).astype(BF16)

    stage_halo(0)
    pl.semaphore_wait(barrier, greeted + len(others))
    send_halo(0)
    farthest = ring // 2
    if farthest >= 2:
        pass_word(2)

    for i in (3, 6, 5, 4):
        inputs[i].wait()
    teacher = jnp.exp(teacher_ref[...].astype(F32))
    target = teacher / jnp.sum(teacher, axis=0, keepdims=True)
    where = point_ref[...]
    spread = (
        (where // 256) * 256 + (where // 32) % 4 * 64
        + (where // 128) % 2 * 32 + where % 32
    )
    voxel = lax.broadcasted_iota(jnp.int32, (512, 1024), 0)
    hits = jnp.where(voxel == spread, 1.0, 0.0).astype(BF16)
    stack = jnp.concatenate([*split3(target), jnp.ones((16, 1024), BF16)], axis=0)
    sums = lax.dot_general(stack, hits, NT, preferred_element_type=F32)
    target_sum = sums[0:16] + (sums[16:32] + sums[32:48])
    points = sums[48:64]

    for steps in range(2, farthest):
        await_word(steps)
        pass_word(steps + 1)

    for k in range(27):
        lane = 128 * (k % 9)
        weight_t[k // 9, :, lane : lane + 128] = weight[k]

    take_halo(0)
    fill_columns(columns, False)

    pre = jnp.zeros((512, 128), F32)
    for q in range(3):
        pre += jnp.dot(
            columns[64 * q : 64 * q + 512, :],
            weight[9 * q : 9 * q + 9].reshape(1152, 128),
            preferred_element_type=F32,
        )
    occupied = occ_cells[...].reshape(512, 128)
    logistic = 1.0 / (1.0 + jnp.exp(-pre))
    hidden = (pre * logistic * occupied).astype(BF16)
    slope = logistic * (1.0 + pre * (1.0 - logistic)) * occupied

    logits = lax.dot_general(head_ref[...], hidden, NT, preferred_element_type=F32)
    student = jnp.exp(logits)
    student = student / jnp.sum(student, axis=0, keepdims=True)
    slope_logits = jnp.where(points > 0.0, points * student - target_sum, 0.0)
    head3 = jnp.concatenate([head_ref[...]] * 3, axis=0)
    pieces = jnp.concatenate(split3(slope_logits), axis=0)
    dhidden = lax.dot_general(pieces, head3, TN, preferred_element_type=F32)
    dpre = (dhidden * slope).astype(BF16)

    cells[1:9, 1:9] = dpre.astype(F32).reshape(8, 8, 8, 128)
    stage_halo(1)
    send_halo(1)

    def own_rows(part, side, q):
        return pl.ds(pl.multiple_of(side * 64 + q * part.rows, part.rows), part.rows)

    def pair_copy(part, run):
        start, stop = part.pair_runs[run]
        return remote(
            part.pair_out.at[start:stop], part.pair_in.at[start:stop],
            part.pair_send.at[run], part.pair_recv.at[run], partner,
        )

    def block_at(part, d):
        return (place[part.a1] + d) % part.n1

    def my_term(part, side, q):
        block = terms[part.first : part.first + part.count, own_rows(part, side, q), :]
        return block.reshape(part.tiles * 8, 128)

    for third, part in enumerate(parts):
        term = lax.dot_general(
            columns[64 * third : 64 * third + 512, :], dpre, TN, preferred_element_type=F32
        )
        terms[9 * third : 9 * third + 9] = term.reshape(9, 128, 128)
        for run, (start, stop) in enumerate(part.pair_runs):
            for turn in range(start, stop):
                block = my_term(part, 1 - core, block_at(part, part.far1[turn]))
                part.pair_out[turn] = block.astype(BF16)
            pair_copy(part, run).start()

    def ring_copy(part, d):
        return remote(
            part.ring_out.at[d], part.ring_in.at[d],
            part.ring_send.at[d], part.ring_recv.at[d], peers[part.a1][d],
        )

    def paired(part, turn):
        for run, (start, stop) in enumerate(part.pair_runs):
            if start == turn:
                pair_copy(part, run).wait_recv()
        own = my_term(part, core, block_at(part, part.far1[turn]))
        return own + part.pair_in[turn].astype(F32)

    if farthest >= 2:
        await_word(farthest)
    for turn in range(max(part.n1 for part in parts) - 1):
        for part in parts:
            if turn < part.n1 - 1:
                d = part.far1[turn]
                part.ring_out[d] = paired(part, turn).astype(BF16)
                ring_copy(part, d).start()
    for part in parts:
        own = paired(part, part.n1 - 1)
        part.mid[0 : part.tiles] = own.reshape(part.tiles, 8, 128)
        spare = part.per * part.n2 - part.tiles
        if spare:
            part.mid[part.tiles :] = jnp.zeros((spare, 8, 128), F32)

    take_halo(1)
    fill_columns(columns_g, True)
    back = jnp.zeros((512, 128), F32)
    for q in range(3):
        back += lax.dot_general(
            columns_g[64 * (2 - q) : 64 * (2 - q) + 512, :], weight_t[q], NT,
            preferred_element_type=F32,
        )
    back = (back * occ_cells[...].reshape(512, 128)).reshape(8, 8, 8, 128)
    for slot in range(4):
        i, j = slot // 2, slot % 2
        block = back[4 * i : 4 * i + 4, 4 * j : 4 * j + 4]
        grad_ref[slot] = block.reshape(128, 128).astype(BF16)

    def mid_copy(part, d):
        p = (place[part.a2] + d) % part.n2
        return remote(
            part.mid.at[pl.ds(p * part.per, part.per)], part.mid_in.at[d],
            part.mid_send.at[d], part.mid_recv.at[d], peers[part.a2][d],
        )

    last_first = (parts[2], parts[0], parts[1])
    for part in last_first:
        block = part.mid[0 : part.tiles]
        for d in reversed(far_first(part.n1)):
            ring_copy(part, d).wait_recv()
            block = block + part.ring_in[d].astype(F32).reshape(part.tiles, 8, 128)
        part.mid[0 : part.tiles] = block
        for d in far_first(part.n2):
            mid_copy(part, d).start()

    def row_copy(part, d):
        return remote(
            part.row_out, part.row_in.at[place[part.a3]],
            part.row_send.at[d], part.row_recv.at[d], peers[part.a3][d],
        )

    for part in last_first:
        block = part.mid[pl.ds(place[part.a2] * part.per, part.per)]
        for d in reversed(far_first(part.n2)):
            mid_copy(part, d).wait_recv()
            block = block + part.mid_in[d]
        block = block.reshape(part.per * 8, 128)
        part.row_out[...] = block
        for d in far_first(part.n3):
            row_copy(part, d).start()
        part.row_in[place[part.a3]] = block

    def thin_copy(part, slot):
        return remote(
            part.full.at[core, 0, 0], part.full.at[core, 0, slot],
            part.thin_send.at[slot], part.thin_recv.at[slot],
            peers[part.a2][part.near2[slot]],
        )

    def wide_copy(part, slot):
        return remote(
            part.full.at[core, 0], part.full.at[core, slot],
            part.wide_send.at[slot], part.wide_recv.at[slot],
            peers[part.a1][part.near1[slot]],
        )

    def core_copy(part, run):
        start, stop = part.core_runs[run]
        block = part.full.at[core, start:stop]
        return remote(
            block, block, part.core_send.at[run], part.core_recv.at[run], partner
        )

    for part in parts:
        for d in reversed(far_first(part.n3)):
            row_copy(part, d).wait_recv()
        total = part.row_in[0]
        for x in range(1, part.n3):
            total = total + part.row_in[x]
        part.full[core, 0, 0] = total.astype(BF16)
        for slot in reversed(range(1, part.n2)):
            thin_copy(part, slot).start()
    for part in parts:
        for slot in range(1, part.n2):
            thin_copy(part, slot).wait_recv()
        for slot in reversed(range(1, part.n1)):
            wide_copy(part, slot).start()
    for run in range(max(len(part.core_runs) for part in parts)):
        for part in parts:
            if run < len(part.core_runs):
                start, stop = part.core_runs[run]
                for slot in range(max(start, 1), stop):
                    wide_copy(part, slot).wait_recv()
                core_copy(part, run).start()

    for other in range(2):
        side = 1 - core if other else core
        for part in parts:
            if other:
                for run in range(len(part.core_runs)):
                    core_copy(part, run).wait_recv()
            homes = [
                (place[part.a2] + part.n2 - d) % part.n2 * part.per for d in part.near2
            ]
            for block_slot in range(part.n1):
                for slot in range(part.n2):
                    piece = part.full[side, block_slot, slot].astype(F32)
                    part.tiles_ref[pl.ds(homes[slot], part.per)] = piece.reshape(
                        part.per, 8, 128
                    )
                block = part.tiles_ref[0 : part.tiles]
                q = block_at(part, part.n1 - part.near1[block_slot])
                part.squares[side, q] = jnp.sum(block * block, axis=0)
                rows = own_rows(part, side, q)
                sum_ref[part.first : part.first + part.count, rows, :] = block.reshape(
                    part.count, part.rows, 128
                )
    squares = sum(jnp.sum(part.squares[...], axis=(0, 1)) for part in parts)
    mean = jnp.full((8, 128), jnp.sum(squares) / (27 * 128 * 128), F32)
    norm_ref[...] = 1.0 / jnp.sqrt(mean + 1e-06)

    for turn in range(2):
        for index in range(8):
            pl.when(leads[index])(halo_copy(turn, index).wait_send)
    for part in parts:
        for run in range(len(part.pair_runs)):
            pair_copy(part, run).wait_send()
        for run in range(len(part.core_runs)):
            core_copy(part, run).wait_send()
        for d in range(1, part.n1):
            ring_copy(part, d).wait_send()
            wide_copy(part, d).wait_send()
        for d in range(1, part.n2):
            mid_copy(part, d).wait_send()
            thin_copy(part, d).wait_send()
        for d in range(1, part.n3):
            row_copy(part, d).wait_send()


def finish_kernel(grad_ref, sum_ref, norm_ref, grad_out, sum_out, staged, sems):
    grad_copy = pltpu.make_async_copy(grad_ref, grad_out, sems.at[9])
    grad_copy.start()
    norm = norm_ref[...].reshape(1, 1, 8, 128)
    copies = []
    for step in range(9):
        span = slice(3 * step, 3 * step + 3)
        block = sum_ref[span].reshape(3, 16, 8, 128) * norm
        staged[span] = block.reshape(3, 128, 128)
        copies.append(pltpu.make_async_copy(staged.at[span], sum_out.at[span], sems.at[step]))
        copies[-1].start()
    for copy in copies:
        copy.wait()
    grad_copy.wait()


def on_device(sizes, features, occupancy, neighbors, point_voxel, conv_weight, head_weight, teacher):
    nx, ring = sizes
    parts = make_parts(nx, ring)
    dma = pltpu.SemaphoreType.DMA
    vmem = pl.BlockSpec(memory_space=pltpu.VMEM)
    hbm = pl.BlockSpec(memory_space=pltpu.HBM)
    args = (
        neighbors.T, occupancy, features, point_voxel.reshape(1, -1), conv_weight,
        head_weight, teacher,
    )
    own = [scratch_of(part) for part in parts]
    names = ["tiles_ref" if name == "tiles" else name for name in own[0]]
    grad, summed, norm = pl.pallas_call(
        functools.partial(kernel, sizes, names),
        out_shape=(
            jax.ShapeDtypeStruct((4, 128, 128), BF16),
            jax.ShapeDtypeStruct((27, 128, 128), F32),
            jax.ShapeDtypeStruct((8, 128), F32),
        ),
        in_specs=[hbm] * 7,
        out_specs=(vmem, vmem, vmem),
        scratch_shapes=[
            *(pltpu.VMEM(arg.shape, arg.dtype) for arg in args),
            dma((7,)),
            pltpu.VMEM((10, 10, 8, 128), F32),
            pltpu.VMEM((8, 8, 8, 128), F32),
            pltpu.VMEM((640, 1152), BF16),
            pltpu.VMEM((640, 1152), BF16),
            pltpu.VMEM((3, 128, 1152), BF16),
            pltpu.VMEM((2, 8, 64, 128), BF16),
            pltpu.VMEM((2, 8, 64, 128), BF16),
            pltpu.VMEM((27, 128, 128), F32),
            dma((2, 8)), dma((2, 8)),
            pltpu.SemaphoreType.REGULAR((2, 2, ring // 2 + 1)),
            *(shape for table in own for shape in table.values()),
        ],
        compiler_params=pltpu.CompilerParams(
            collective_id=0, has_side_effects=True, vmem_limit_bytes=48 * 1024 * 1024
        ),
    )(*(pltpu.with_memory_space_constraint(arg, pltpu.HBM) for arg in args))
    return pl.pallas_call(
        finish_kernel,
        out_shape=(
            jax.ShapeDtypeStruct((4, 128, 128), BF16),
            jax.ShapeDtypeStruct((27, 128, 128), F32),
        ),
        in_specs=[vmem, vmem, vmem],
        out_specs=(hbm, hbm),
        scratch_shapes=[pltpu.VMEM((27, 128, 128), F32), dma((10,))],
        compiler_params=pltpu.CompilerParams(vmem_limit_bytes=16 * 1024 * 1024),
    )(grad, summed, norm)


def solution(mesh):
    ring = mesh.shape["ty"] // 2
    nx = mesh.shape["tx"] // ring
    in_specs = (
        P(("tx", "ty"), None, None),
        P(("tx", "ty"), None),
        P(None, ("tx", "ty")),
        P(("tx", "ty")),
        P(),
        P(),
        P(None, ("tx", "ty")),
    )
    out_specs = (P(("tx", "ty"), None, None), P())
    return jax.shard_map(
        functools.partial(on_device, (nx, ring)),
        mesh=mesh, in_specs=in_specs, out_specs=out_specs, check_vma=False,
    )
```

```python
import functools

import jax
import jax.numpy as jnp
from jax import lax
from jax.experimental import pallas as pl
from jax.experimental.pallas import tpu as pltpu
from jax.sharding import PartitionSpec as P

F32 = jnp.float32
BF16 = jnp.bfloat16
MESH = pl.DeviceIdType.MESH
ROUTES = ((-1, 0), (1, 0), (0, -1), (0, 1), (-1, -1), (-1, 1), (1, -1), (1, 1))
TN = (((0,), (0,)), ((), ()))
NT = (((1,), (1,)), ((), ()))
PARTS = ((0, 8, "yzx"), (8, 8, "zyx"), (16, 11, "xyz"))


def far_first(n):
    return sorted(range(1, n), key=lambda d: (-min(d, n - d), d))


def near_first(n):
    return sorted(range(n), key=lambda d: (min(d, n - d), d))


def runs(n, *cuts):
    edges = sorted({0, n, *(cut for cut in cuts if cut < n)})
    return list(zip(edges, edges[1:]))


class Part:
    def __init__(self, place, first, count, axes, size):
        self.index = place
        self.first, self.count = first, count
        self.a1, self.a2, self.a3 = axes
        self.n1, self.n2, self.n3 = (size[axis] for axis in axes)
        self.rows = 64 // self.n1
        self.tiles = count * self.rows // 8
        self.per = -(-self.tiles // self.n2)
        self.far1 = far_first(self.n1) + [0]
        self.near1 = near_first(self.n1)
        self.near2 = near_first(self.n2)
        self.pair_runs = runs(self.n1)
        self.core_runs = runs(self.n1)


def make_parts(nx, ring):
    size = {"x": nx, "y": ring, "z": ring}
    return [Part(i, *spec, size) for i, spec in enumerate(PARTS)]


def scratch_of(part):
    dma = pltpu.SemaphoreType.DMA
    wide = pltpu.VMEM((part.n1, part.tiles * 8, 128), BF16)
    return {
        "pair_out": wide, "pair_in": wide, "ring_out": wide, "ring_in": wide,
        "mid": pltpu.VMEM((part.n2 * part.per, 8, 128), F32),
        "mid_in": pltpu.VMEM((part.n2, part.per, 8, 128), F32),
        "row_out": pltpu.VMEM((part.per * 8, 128), F32),
        "row_in": pltpu.VMEM((part.n3, part.per * 8, 128), F32),
        "full": pltpu.VMEM((2, part.n1, part.n2, part.per * 8, 128), BF16),
        "tiles": pltpu.VMEM((part.n2 * part.per, 8, 128), F32),
        "squares": pltpu.VMEM((2, part.n1, 8, 128), F32),
        "pair_send": dma((len(part.pair_runs),)), "pair_recv": dma((len(part.pair_runs),)),
        "ring_send": dma((part.n1,)), "ring_recv": dma((part.n1,)),
        "mid_send": dma((part.n2,)), "mid_recv": dma((part.n2,)),
        "row_send": dma((part.n3,)), "row_recv": dma((part.n3,)),
        "thin_send": dma((part.n2,)), "thin_recv": dma((part.n2,)),
        "wide_send": dma((part.n1,)), "wide_recv": dma((part.n1,)),
        "core_send": dma((len(part.core_runs),)), "core_recv": dma((len(part.core_runs),)),
    }


def span_to_send(step):
    if step < 0:
        return slice(1, 2)
    if step > 0:
        return slice(8, 9)
    return slice(1, 9)


def span_received(step):
    if step < 0:
        return slice(9, 10)
    if step > 0:
        return slice(0, 1)
    return slice(1, 9)


def split3(value):
    one = value.astype(BF16)
    rest = value - one.astype(F32)
    two = rest.astype(BF16)
    three = (rest - two.astype(F32)).astype(BF16)
    return one, two, three


def kernel(sizes, names, *refs):
    nx, ring = sizes
    parts = make_parts(nx, ring)
    in_hbm, (grad_ref, sum_ref, norm_ref) = refs[:7], refs[7:10]
    (
        near_ref, occ_ref, feat_ref, point_ref, weight, head_ref, teacher_ref, input_sem,
        cells, occ_cells, columns, columns_g, weight_t, halo_out, halo_in, terms,
        halo_send, halo_recv, word_sem,
    ) = refs[10:29]
    rest = iter(refs[29:])
    for part in parts:
        for name in names:
            setattr(part, name, next(rest))

    n_tx, n_ty = nx * ring, 2 * ring
    tx = lax.axis_index("tx")
    ty = lax.axis_index("ty")
    core = ty % 2
    place = {"x": tx // ring, "z": tx % ring, "y": ty // 2}
    extent = {"x": nx, "y": ring, "z": ring}

    def along(axis, d):
        if axis == "x":
            return (((place["x"] + d) % nx) * ring + place["z"], ty)
        if axis == "z":
            return (place["x"] * ring + (place["z"] + d) % ring, ty)
        return (tx, ((place["y"] + d) % ring) * 2 + core)

    peers = {axis: [along(axis, d) for d in range(extent[axis])] for axis in "xyz"}
    partner = (tx, place["y"] * 2 + 1 - core)

    def toward(route):
        ex, ey = route
        return ((tx + ex + n_tx) % n_tx, (ty + ey + n_ty) % n_ty)

    def remote(src, dst, send, recv, device):
        return pltpu.make_async_remote_copy(
            src_ref=src, dst_ref=dst, send_sem=send, recv_sem=recv,
            device_id=device, device_id_type=MESH,
        )

    barrier = pltpu.get_barrier_semaphore()

    def greet(device):
        pl.semaphore_signal(barrier, inc=1, device_id=device, device_id_type=MESH)

    def on_map(x, y):
        return (x >= 0) & (x < n_tx) & (y >= 0) & (y < n_ty)

    leads = [on_map(tx + ex, ty + ey) for ex, ey in ROUTES]
    comes = [on_map(tx - ex, ty - ey) for ex, ey in ROUTES]
    greeted = 0
    for route, valid in zip(ROUTES, leads):
        pl.when(valid)(functools.partial(greet, toward(route)))
        greeted = greeted + valid.astype(jnp.int32)
    held = (near_ref, occ_ref, feat_ref, point_ref, weight, head_ref, teacher_ref)
    inputs = [
        pltpu.make_async_copy(src, dst, input_sem.at[i])
        for i, (src, dst) in enumerate(zip(in_hbm, held))
    ]
    for i in (0, 1, 2, 3, 6, 5, 4):
        inputs[i].start()
    others = [peers[axis][d] for axis in "yz" for d in (1, ring - 1)]
    others += [partner] + [peers["x"][d] for d in far_first(nx)]
    for device in others:
        greet(device)

    def pass_word(steps):
        for i, axis in enumerate("yz"):
            for way, d in enumerate((1, ring - 1)):
                pl.semaphore_signal(
                    word_sem.at[i, way, steps], inc=1, device_id=peers[axis][d],
                    device_id_type=MESH,
                )

    def await_word(steps):
        for i in range(2):
            for way in range(2):
                pl.semaphore_wait(word_sem.at[i, way, steps], 1)

    for i in (0, 1, 2):
        inputs[i].wait()
    active = (near_ref[:, 13:14] >= 0).astype(jnp.int32)
    occupancy = (occ_ref[...] * active).astype(F32)
    for slot in range(4):
        i, j = slot // 2, slot % 2
        column = jnp.broadcast_to(occupancy[slot : slot + 1, :], (128, 128)).T
        occ_cells[4 * i : 4 * i + 4, 4 * j : 4 * j + 4] = column.reshape(4, 4, 8, 128)
        masked = feat_ref[slot].astype(F32) * column
        cells[1 + 4 * i : 5 + 4 * i, 1 + 4 * j : 5 + 4 * j] = masked.reshape(4, 4, 8, 128)

    def halo_copy(turn, index):
        count = 64 if index < 4 else 16
        return remote(
            halo_out.at[turn, index, 0:count], halo_in.at[turn, index, 0:count],
            halo_send.at[turn, index], halo_recv.at[turn, index], toward(ROUTES[index]),
        )

    def stage_halo(turn):
        for index, (ex, ey) in enumerate(ROUTES):
            block = cells[span_to_send(ex), span_to_send(ey)]
            if index < 4:
                halo_out[turn, index] = block.reshape(64, 128).astype(BF16)
            else:
                block = block.reshape(8, 128)
                halo_out[turn, index, 0:16] = jnp.concatenate([block, block], axis=0).astype(BF16)

    def send_halo(turn):
        for index in (4, 5, 6, 7, 0, 1, 2, 3):
            pl.when(leads[index])(halo_copy(turn, index).start)

    def take_halo(turn):
        for index, (ex, ey) in enumerate(ROUTES):
            pl.when(comes[index])(halo_copy(turn, index).wait_recv)
            if index < 4:
                block = halo_in[turn, index].astype(F32)
                shape = (1, 8, 8, 128) if ex else (8, 1, 8, 128)
            else:
                block = halo_in[turn, index, 0:16].astype(F32)[0:8]
                shape = (1, 1, 8, 128)
            block = jnp.where(comes[index], block, 0.0)
            cells[span_received(ex), span_received(ey)] = block.reshape(shape)

    layer = lax.broadcasted_iota(jnp.int32, (80, 8, 128), 1)

    def fill_columns(target, flip):
        for dy in range(3):
            start = 2 - dy if flip else dy
            block = cells[:, start : start + 8].reshape(80, 8, 128)
            for dz in range(3):
                move = 1 - dz if flip else dz - 1
                if move > 0:
                    shifted = jnp.where(layer == 7, 0.0, pltpu.roll(block, 7, 1))
                elif move < 0:
                    shifted = jnp.where(layer == 0, 0.0, pltpu.roll(block, 1, 1))
                else:
                    shifted = block
                lane = 128 * (3 * dy + dz)
                target[:, lane : lane + 128] = shifted.reshape(640, 128).astype(BF16)

    stage_halo(0)
    pl.semaphore_wait(barrier, greeted + len(others))
    send_halo(0)
    farthest = ring // 2
    if farthest >= 2:
        pass_word(2)

    for i in (3, 6, 5, 4):
        inputs[i].wait()
    teacher = jnp.exp(teacher_ref[...].astype(F32))
    target = teacher / jnp.sum(teacher, axis=0, keepdims=True)
    where = point_ref[...]
    spread = (
        (where // 256) * 256 + (where // 32) % 4 * 64
        + (where // 128) % 2 * 32 + where % 32
    )
    voxel = lax.broadcasted_iota(jnp.int32, (512, 1024), 0)
    hits = jnp.where(voxel == spread, 1.0, 0.0).astype(BF16)
    stack = jnp.concatenate([*split3(target), jnp.ones((16, 1024), BF16)], axis=0)
    sums = lax.dot_general(stack, hits, NT, preferred_element_type=F32)
    target_sum = sums[0:16] + (sums[16:32] + sums[32:48])
    points = sums[48:64]

    for steps in range(2, farthest):
        await_word(steps)
        pass_word(steps + 1)

    for k in range(27):
        lane = 128 * (k % 9)
        weight_t[k // 9, :, lane : lane + 128] = weight[k]

    take_halo(0)
    fill_columns(columns, False)

    pre = jnp.zeros((512, 128), F32)
    for q in range(3):
        pre += jnp.dot(
            columns[64 * q : 64 * q + 512, :],
            weight[9 * q : 9 * q + 9].reshape(1152, 128),
            preferred_element_type=F32,
        )
    occupied = occ_cells[...].reshape(512, 128)
    logistic = 1.0 / (1.0 + jnp.exp(-pre))
    hidden = (pre * logistic * occupied).astype(BF16)
    slope = logistic * (1.0 + pre * (1.0 - logistic)) * occupied

    logits = lax.dot_general(head_ref[...], hidden, NT, preferred_element_type=F32)
    student = jnp.exp(logits)
    student = student / jnp.sum(student, axis=0, keepdims=True)
    slope_logits = jnp.where(points > 0.0, points * student - target_sum, 0.0)
    head3 = jnp.concatenate([head_ref[...]] * 3, axis=0)
    pieces = jnp.concatenate(split3(slope_logits), axis=0)
    dhidden = lax.dot_general(pieces, head3, TN, preferred_element_type=F32)
    dpre = (dhidden * slope).astype(BF16)

    cells[1:9, 1:9] = dpre.astype(F32).reshape(8, 8, 8, 128)
    stage_halo(1)
    send_halo(1)

    def own_rows(part, side, q):
        return pl.ds(pl.multiple_of(side * 64 + q * part.rows, part.rows), part.rows)

    def pair_copy(part, run):
        start, stop = part.pair_runs[run]
        return remote(
            part.pair_out.at[start:stop], part.pair_in.at[start:stop],
            part.pair_send.at[run], part.pair_recv.at[run], partner,
        )

    def block_at(part, d):
        return (place[part.a1] + d) % part.n1

    def my_term(part, side, q):
        block = terms[part.first : part.first + part.count, own_rows(part, side, q), :]
        return block.reshape(part.tiles * 8, 128)

    for third, part in enumerate(parts):
        term = lax.dot_general(
            columns[64 * third : 64 * third + 512, :], dpre, TN, preferred_element_type=F32
        )
        terms[9 * third : 9 * third + 9] = term.reshape(9, 128, 128)
        for run, (start, stop) in enumerate(part.pair_runs):
            for turn in range(start, stop):
                block = my_term(part, 1 - core, block_at(part, part.far1[turn]))
                part.pair_out[turn] = block.astype(BF16)
            pair_copy(part, run).start()

    def ring_copy(part, d):
        return remote(
            part.ring_out.at[d], part.ring_in.at[d],
            part.ring_send.at[d], part.ring_recv.at[d], peers[part.a1][d],
        )

    def paired(part, turn):
        for run, (start, stop) in enumerate(part.pair_runs):
            if start == turn:
                pair_copy(part, run).wait_recv()
        own = my_term(part, core, block_at(part, part.far1[turn]))
        return own + part.pair_in[turn].astype(F32)

    if farthest >= 2:
        await_word(farthest)
    for turn in range(max(part.n1 for part in parts) - 1):
        for part in parts:
            if turn < part.n1 - 1:
                d = part.far1[turn]
                part.ring_out[d] = paired(part, turn).astype(BF16)
                ring_copy(part, d).start()
    for part in parts:
        own = paired(part, part.n1 - 1)
        part.mid[0 : part.tiles] = own.reshape(part.tiles, 8, 128)
        spare = part.per * part.n2 - part.tiles
        if spare:
            part.mid[part.tiles :] = jnp.zeros((spare, 8, 128), F32)

    def mid_copy(part, d):
        p = (place[part.a2] + d) % part.n2
        return remote(
            part.mid.at[pl.ds(p * part.per, part.per)], part.mid_in.at[d],
            part.mid_send.at[d], part.mid_recv.at[d], peers[part.a2][d],
        )

    last_first = (parts[2], parts[0], parts[1])
    for part in last_first:
        block = part.mid[0 : part.tiles]
        for d in reversed(far_first(part.n1)):
            ring_copy(part, d).wait_recv()
            block = block + part.ring_in[d].astype(F32).reshape(part.tiles, 8, 128)
        part.mid[0 : part.tiles] = block
        for d in far_first(part.n2):
            mid_copy(part, d).start()

    take_halo(1)
    fill_columns(columns_g, True)
    back = jnp.zeros((512, 128), F32)
    for q in range(3):
        back += lax.dot_general(
            columns_g[64 * (2 - q) : 64 * (2 - q) + 512, :], weight_t[q], NT,
            preferred_element_type=F32,
        )
    back = (back * occ_cells[...].reshape(512, 128)).reshape(8, 8, 8, 128)
    for slot in range(4):
        i, j = slot // 2, slot % 2
        block = back[4 * i : 4 * i + 4, 4 * j : 4 * j + 4]
        grad_ref[slot] = block.reshape(128, 128).astype(BF16)

    def row_copy(part, d):
        return remote(
            part.row_out, part.row_in.at[place[part.a3]],
            part.row_send.at[d], part.row_recv.at[d], peers[part.a3][d],
        )

    for part in last_first:
        block = part.mid[pl.ds(place[part.a2] * part.per, part.per)]
        for d in reversed(far_first(part.n2)):
            mid_copy(part, d).wait_recv()
            block = block + part.mid_in[d]
        block = block.reshape(part.per * 8, 128)
        part.row_out[...] = block
        for d in far_first(part.n3):
            row_copy(part, d).start()
        part.row_in[place[part.a3]] = block

    def thin_copy(part, slot):
        return remote(
            part.full.at[core, 0, 0], part.full.at[core, 0, slot],
            part.thin_send.at[slot], part.thin_recv.at[slot],
            peers[part.a2][part.near2[slot]],
        )

    def wide_copy(part, slot):
        return remote(
            part.full.at[core, 0], part.full.at[core, slot],
            part.wide_send.at[slot], part.wide_recv.at[slot],
            peers[part.a1][part.near1[slot]],
        )

    def core_copy(part, run):
        start, stop = part.core_runs[run]
        block = part.full.at[core, start:stop]
        return remote(
            block, block, part.core_send.at[run], part.core_recv.at[run], partner
        )

    for part in parts:
        for d in reversed(far_first(part.n3)):
            row_copy(part, d).wait_recv()
        total = part.row_in[0]
        for x in range(1, part.n3):
            total = total + part.row_in[x]
        part.full[core, 0, 0] = total.astype(BF16)
        for slot in reversed(range(1, part.n2)):
            thin_copy(part, slot).start()
    for part in parts:
        for slot in range(1, part.n2):
            thin_copy(part, slot).wait_recv()
        for slot in reversed(range(1, part.n1)):
            wide_copy(part, slot).start()
    for run in range(max(len(part.core_runs) for part in parts)):
        for part in parts:
            if run < len(part.core_runs):
                start, stop = part.core_runs[run]
                for slot in range(max(start, 1), stop):
                    wide_copy(part, slot).wait_recv()
                core_copy(part, run).start()

    for other in range(2):
        side = 1 - core if other else core
        for part in parts:
            if other:
                for run in range(len(part.core_runs)):
                    core_copy(part, run).wait_recv()
            homes = [
                (place[part.a2] + part.n2 - d) % part.n2 * part.per for d in part.near2
            ]
            for block_slot in range(part.n1):
                for slot in range(part.n2):
                    piece = part.full[side, block_slot, slot].astype(F32)
                    part.tiles_ref[pl.ds(homes[slot], part.per)] = piece.reshape(
                        part.per, 8, 128
                    )
                block = part.tiles_ref[0 : part.tiles]
                q = block_at(part, part.n1 - part.near1[block_slot])
                part.squares[side, q] = jnp.sum(block * block, axis=0)
                rows = own_rows(part, side, q)
                sum_ref[part.first : part.first + part.count, rows, :] = block.reshape(
                    part.count, part.rows, 128
                )
    squares = sum(jnp.sum(part.squares[...], axis=(0, 1)) for part in parts)
    mean = jnp.full((8, 128), jnp.sum(squares) / (27 * 128 * 128), F32)
    norm_ref[...] = 1.0 / jnp.sqrt(mean + 1e-06)

    for turn in range(2):
        for index in range(8):
            pl.when(leads[index])(halo_copy(turn, index).wait_send)
    for part in parts:
        for run in range(len(part.pair_runs)):
            pair_copy(part, run).wait_send()
        for run in range(len(part.core_runs)):
            core_copy(part, run).wait_send()
        for d in range(1, part.n1):
            ring_copy(part, d).wait_send()
            wide_copy(part, d).wait_send()
        for d in range(1, part.n2):
            mid_copy(part, d).wait_send()
            thin_copy(part, d).wait_send()
        for d in range(1, part.n3):
            row_copy(part, d).wait_send()


def finish_kernel(grad_ref, sum_ref, norm_ref, grad_out, sum_out, staged, sems):
    grad_copy = pltpu.make_async_copy(grad_ref, grad_out, sems.at[9])
    grad_copy.start()
    norm = norm_ref[...].reshape(1, 1, 8, 128)
    copies = []
    for step in range(9):
        span = slice(3 * step, 3 * step + 3)
        block = sum_ref[span].reshape(3, 16, 8, 128) * norm
        staged[span] = block.reshape(3, 128, 128)
        copies.append(pltpu.make_async_copy(staged.at[span], sum_out.at[span], sems.at[step]))
        copies[-1].start()
    for copy in copies:
        copy.wait()
    grad_copy.wait()


def on_device(sizes, features, occupancy, neighbors, point_voxel, conv_weight, head_weight, teacher):
    nx, ring = sizes
    parts = make_parts(nx, ring)
    dma = pltpu.SemaphoreType.DMA
    vmem = pl.BlockSpec(memory_space=pltpu.VMEM)
    hbm = pl.BlockSpec(memory_space=pltpu.HBM)
    args = (
        neighbors.T, occupancy, features, point_voxel.reshape(1, -1), conv_weight,
        head_weight, teacher,
    )
    own = [scratch_of(part) for part in parts]
    names = ["tiles_ref" if name == "tiles" else name for name in own[0]]
    grad, summed, norm = pl.pallas_call(
        functools.partial(kernel, sizes, names),
        out_shape=(
            jax.ShapeDtypeStruct((4, 128, 128), BF16),
            jax.ShapeDtypeStruct((27, 128, 128), F32),
            jax.ShapeDtypeStruct((8, 128), F32),
        ),
        in_specs=[hbm] * 7,
        out_specs=(vmem, vmem, vmem),
        scratch_shapes=[
            *(pltpu.VMEM(arg.shape, arg.dtype) for arg in args),
            dma((7,)),
            pltpu.VMEM((10, 10, 8, 128), F32),
            pltpu.VMEM((8, 8, 8, 128), F32),
            pltpu.VMEM((640, 1152), BF16),
            pltpu.VMEM((640, 1152), BF16),
            pltpu.VMEM((3, 128, 1152), BF16),
            pltpu.VMEM((2, 8, 64, 128), BF16),
            pltpu.VMEM((2, 8, 64, 128), BF16),
            pltpu.VMEM((27, 128, 128), F32),
            dma((2, 8)), dma((2, 8)),
            pltpu.SemaphoreType.REGULAR((2, 2, ring // 2 + 1)),
            *(shape for table in own for shape in table.values()),
        ],
        compiler_params=pltpu.CompilerParams(
            collective_id=0, has_side_effects=True, vmem_limit_bytes=48 * 1024 * 1024
        ),
    )(*(pltpu.with_memory_space_constraint(arg, pltpu.HBM) for arg in args))
    return pl.pallas_call(
        finish_kernel,
        out_shape=(
            jax.ShapeDtypeStruct((4, 128, 128), BF16),
            jax.ShapeDtypeStruct((27, 128, 128), F32),
        ),
        in_specs=[vmem, vmem, vmem],
        out_specs=(hbm, hbm),
        scratch_shapes=[pltpu.VMEM((27, 128, 128), F32), dma((10,))],
        compiler_params=pltpu.CompilerParams(vmem_limit_bytes=16 * 1024 * 1024),
    )(grad, summed, norm)


def solution(mesh):
    ring = mesh.shape["ty"] // 2
    nx = mesh.shape["tx"] // ring
    in_specs = (
        P(("tx", "ty"), None, None),
        P(("tx", "ty"), None),
        P(None, ("tx", "ty")),
        P(("tx", "ty")),
        P(),
        P(),
        P(None, ("tx", "ty")),
    )
    out_specs = (P(("tx", "ty"), None, None), P())
    return jax.shard_map(
        functools.partial(on_device, (nx, ring)),
        mesh=mesh, in_specs=in_specs, out_specs=out_specs, check_vma=False,
    )
```
